32 devices in a mesh: gy: 4 (over z), gz: 8 (over y, x, core).
Axes of the slice: x: 2, y: 2, z: 4, core: 2. Of those that a mesh axis runs over, the one named last changes fastest.
Arguments:
- data_weight: float32 [320, 160, 640], P('gy', 'gz'), may hold values from 0.25 to 4
- blob_taps: float32 [3, 7], replicated, may hold values from 0.2 to 1
Outputs:
- new_weight: float32 [320, 160, 640], P('gy', 'gz')
- changes: float32 [3], replicated
The draws below stay inside these ranges and needn't reach their ends.
All inputs are finite; a program needn't handle non-finite values.
Results may differ from the reference program's by a relative error of at most 0.00002.
Values sent between devices are 32-bit elements; how exact they have to be, the bound alone decides.
No kernel may reach another device: no remote copies, remote signals or barrier semaphores. Data moves between devices by JAX's collectives and lax.ppermute only.
A program may use at most 64 MiB of HBM per device.

```python
import math
import jax
import jax.numpy as jnp
from jax import lax

XLEN = 640
RAD = 3
TAPS = 7
ITERS = 3
YLEN = 320
ZLEN = 160


def level_of(key, extent, shards, least, largest):
    gain = 1.0
    for axis_at, parts in shards:
        heights = jax.random.uniform(jax.random.fold_in(jax.random.fold_in(key, 6), axis_at), (parts,), jnp.float32, least / len(shards), largest / len(shards))
        gain = gain * jnp.repeat(jnp.exp(heights), extent[axis_at] // parts).reshape((-1,) + (1,) * (len(extent) - 1 - axis_at))
    return gain


def setup_inputs(seed: int = 0) -> dict:
    arg_keys = jax.random.split(jax.random.key(seed), 3)
    return {
        "data_weight": jnp.clip(jnp.exp(math.log(4.0) - 2.7725887 * jax.random.uniform(arg_keys[0], (YLEN, ZLEN, XLEN), jnp.float32) ** level_of(arg_keys[0], (YLEN, ZLEN, XLEN), ((0, 4), (1, 8)), -0.2, 0.2)), 0.25, 4.0),
        "blob_taps": jnp.clip(jax.random.uniform(arg_keys[1], (3, TAPS), jnp.float32, 0.2, 1.0), 0.2, 1.0),
    }


def smear_axis(field, kernel, axis_dim):
    length = field.shape[axis_dim]
    widths = [(0, 0), (0, 0), (0, 0)]
    widths[axis_dim] = (RAD, RAD)
    padded = jnp.pad(field, widths)
    result = jnp.zeros_like(field)
    for offset in range(2 * RAD + 1):
        result = result + kernel[offset] * lax.slice_in_dim(padded, offset, offset + length, axis=axis_dim)
    return result


def reference(data_weight, blob_taps):
    kernel = blob_taps / jnp.sum(blob_taps, axis=1, keepdims=True)
    weight = jnp.ones_like(data_weight)
    changes = []
    for iteration in range(ITERS):
        product = weight * data_weight
        blurred = smear_axis(product, kernel[2], 2)
        blurred = smear_axis(blurred, kernel[0], 0)
        blurred = smear_axis(blurred, kernel[1], 1)
        weight = weight / blurred
        changes.append(jnp.max(jnp.abs(blurred - 1.0)))
    return weight, jnp.stack(changes)
```

```python
import functools

import jax
import jax.numpy as jnp
from jax import lax
from jax.experimental import pallas as pl
from jax.experimental.pallas import tpu as pltpu
from jax.sharding import PartitionSpec as P

RAD = 3
ITERS = 3
LANES = 128
ROWS = 8


def smear_x(row, taps):
    length = row.shape[1]
    padded = jnp.concatenate([row, jnp.zeros((row.shape[0], LANES), row.dtype)], axis=1)
    total = length + LANES
    result = taps[RAD] * row
    for k in range(2 * RAD + 1):
        if k != RAD:
            moved = pltpu.roll(padded, (RAD - k) % total, 1)
            result = result + taps[k] * moved[:, :length]
    return result


def smear_x_all(src, dst, taps):
    planes, height, _ = src.shape
    chunk = 2 * ROWS if height % (2 * ROWS) == 0 else ROWS

    def body(z, _):
        for y in range(0, height, chunk):
            dst[z, y : y + chunk, :] = smear_x(src[z, y : y + chunk, :], taps)
        return 0

    lax.fori_loop(0, planes, body, 0)


def first_kernel(kernel_ref, d_ref, u_ref):
    taps = [kernel_ref[2, k] for k in range(2 * RAD + 1)]
    smear_x_all(d_ref, u_ref, taps)


def step_kernel(last, *refs):
    if last:
        kernel_ref, p_ref, u_ref, zlo_ref, zhi_ref, tail_ref, d_ref, out_ref, dev_ref, ext = refs
    else:
        kernel_ref, p_ref, u_ref, zlo_ref, zhi_ref, tail_ref, out_ref, unext_ref, dev_ref, ext = refs
    planes, height, length = p_ref.shape
    ntaps = 2 * RAD + 1
    ky = [kernel_ref[0, k] for k in range(ntaps)]
    kz = [kernel_ref[1, k] for k in range(ntaps)]
    total = height + ROWS

    def fill(z, _):
        ext[z + RAD, 0:height, :] = u_ref[z]
        return 0

    lax.fori_loop(0, planes, fill, 0)

    def fill_tail(z, _):
        ext[z, height:total, :] = tail_ref[z]
        return 0

    lax.fori_loop(0, planes + 2 * RAD, fill_tail, 0)
    for z in range(RAD):
        ext[z, 0:height, :] = zlo_ref[z]
        ext[planes + RAD + z, 0:height, :] = zhi_ref[z]

    dev_ref[...] = jnp.zeros_like(dev_ref)
    for x in range(0, length, LANES):
        cols = slice(x, x + LANES)

        def body(z, _, cols=cols):
            v = kz[0] * ext[z, :, cols]
            for k in range(1, ntaps):
                v = v + kz[k] * ext[z + k, :, cols]
            b = ky[RAD] * v[:height]
            for k in range(ntaps):
                if k != RAD:
                    b = b + ky[k] * pltpu.roll(v, (RAD - k) % total, 0)[:height]
            p = p_ref[z, :, cols]
            if last:
                out_ref[z, :, cols] = p / (b * d_ref[z, :, cols])
            else:
                out_ref[z, :, cols] = p / b
            off = jnp.max(jnp.abs(b - 1.0).reshape(height // ROWS, ROWS, LANES), axis=0)
            dev_ref[...] = jnp.maximum(dev_ref[...], off)
            return 0

        lax.fori_loop(0, planes, body, 0)
    if not last:
        smear_x_all(out_ref, unext_ref, [kernel_ref[2, k] for k in range(ntaps)])


def exchange(u):
    ny = lax.axis_size("gy")
    nz = lax.axis_size("gz")
    planes, height, _ = u.shape

    def move(block, dy, dz):
        pairs = []
        for y in range(ny):
            for z in range(nz):
                if 0 <= y + dy < ny and 0 <= z + dz < nz:
                    pairs.append(((y + dy) * nz + z + dz, y * nz + z))
        return lax.ppermute(block, ("gy", "gz"), pairs)

    lo = slice(0, RAD)
    zend = slice(planes - RAD, planes)
    yend = slice(height - RAD, height)
    zlo = move(u[zend], 0, -1)
    zhi = move(u[lo], 0, 1)
    ylo = jnp.concatenate(
        [move(u[zend, yend], -1, -1), move(u[:, yend], -1, 0), move(u[lo, yend], -1, 1)], axis=0
    )
    yhi = jnp.concatenate(
        [move(u[zend, lo], 1, -1), move(u[:, lo], 1, 0), move(u[lo, lo], 1, 1)], axis=0
    )
    gap = jnp.zeros((ylo.shape[0], ROWS - 2 * RAD, ylo.shape[2]), u.dtype)
    tail = jnp.concatenate([yhi, gap, ylo], axis=1)
    return zlo, zhi, tail


def shards(data_weight, blob_taps):
    kernel = blob_taps / jnp.sum(blob_taps, axis=1, keepdims=True)
    d = jnp.transpose(data_weight, (1, 0, 2))
    planes, height, length = d.shape
    vmem = pl.BlockSpec(memory_space=pltpu.VMEM)
    smem = pl.BlockSpec(memory_space=pltpu.SMEM)
    whole = jax.ShapeDtypeStruct(d.shape, d.dtype)
    dev_shape = jax.ShapeDtypeStruct((ROWS, LANES), d.dtype)
    ext = pltpu.VMEM((planes + 2 * RAD, height + ROWS, length), d.dtype)
    params = pltpu.CompilerParams(vmem_limit_bytes=56 * 1024 * 1024)
    u = pl.pallas_call(
        first_kernel, out_shape=whole, in_specs=[smem, vmem], out_specs=vmem, compiler_params=params, name="first"
    )(kernel, d)
    p = d
    devs = []
    for iteration in range(ITERS):
        last = iteration == ITERS - 1
        zlo, zhi, tail = exchange(u)
        args = [kernel, p, u, zlo, zhi, tail] + ([d] if last else [])
        outs = pl.pallas_call(
            functools.partial(step_kernel, last),
            out_shape=[whole, dev_shape] if last else [whole, whole, dev_shape],
            in_specs=[smem] + [vmem] * (len(args) - 1),
            out_specs=[vmem] * (2 if last else 3),
            scratch_shapes=[ext],
            compiler_params=params,
            name="step",
        )(*args)
        if last:
            weight, dev = outs
        else:
            p, u, dev = outs
        devs.append(dev)
    local = jnp.max(jnp.stack(devs), axis=(1, 2))
    return jnp.transpose(weight, (1, 0, 2)), lax.pmax(local, ("gy", "gz"))


def solution(mesh):
    return jax.shard_map(
        shards,
        mesh=mesh,
        in_specs=(P("gy", "gz", None), P()),
        out_specs=(P("gy", "gz", None), P()),
        check_vma=False,
    )
```

```python
import functools

import jax
import jax.numpy as jnp
from jax import lax
from jax.experimental import pallas as pl
from jax.experimental.pallas import tpu as pltpu
from jax.sharding import PartitionSpec as P

RAD = 3
ITERS = 3
LANES = 128
ROWS = 8


def smear_x(row, taps):
    length = row.shape[1]
    padded = jnp.concatenate([row, jnp.zeros((row.shape[0], LANES), row.dtype)], axis=1)
    total = length + LANES
    result = taps[RAD] * row
    for k in range(2 * RAD + 1):
        if k != RAD:
            moved = pltpu.roll(padded, (RAD - k) % total, 1)
            result = result + taps[k] * moved[:, :length]
    return result


def smear_x_all(src, dst, taps):
    planes, height, _ = src.shape
    chunk = 2 * ROWS if height % (2 * ROWS) == 0 else ROWS

    def body(z, _):
        for y in range(0, height, chunk):
            dst[z, y : y + chunk, :] = smear_x(src[z, y : y + chunk, :], taps)
        return 0

    lax.fori_loop(0, planes, body, 0)


def first_kernel(kernel_ref, d_ref, u_ref):
    taps = [kernel_ref[2, k] for k in range(2 * RAD + 1)]
    smear_x_all(d_ref, u_ref, taps)


def smear_y(column, taps, height):
    result = taps[RAD] * column[:height]
    for k in range(2 * RAD + 1):
        if k != RAD:
            moved = pltpu.roll(column, (RAD - k) % (height + ROWS), 0)
            result = result + taps[k] * moved[:height]
    return result


def taps_of(kernel_ref, row):
    return [kernel_ref[row, k] for k in range(2 * RAD + 1)]


def rim_kernel(kernel_ref, u_ref, ylo_ref, yhi_ref, vtop_ref, vbot_ref, tail_ref):
    planes = tail_ref.shape[0]
    have, height, length = u_ref.shape
    ky = taps_of(kernel_ref, 0)

    def fill(z, _):
        tail_ref[z] = jnp.zeros((ROWS, length), tail_ref.dtype)
        tail_ref[z, 0:RAD, :] = yhi_ref[z]
        tail_ref[z, ROWS - RAD : ROWS, :] = ylo_ref[z]
        return 0

    lax.fori_loop(0, planes, fill, 0)
    for x in range(0, length, LANES):
        cols = slice(x, x + LANES)

        def body(i, _, cols=cols):
            for out, z, t in ((vtop_ref, i, i), (vbot_ref, have - RAD + i, planes - RAD + i)):
                column = jnp.concatenate([u_ref[z, :, cols], tail_ref[t, :, cols]], axis=0)
                out[i, :, cols] = smear_y(column, ky, height)
            return 0

        lax.fori_loop(0, RAD, body, 0)


def finish(v_ref, z, cols, kz, p_ref, pz, d_ref, out_ref, to, dev_ref):
    height = p_ref.shape[1]
    b = kz[0] * v_ref[z, :, cols]
    for k in range(1, 2 * RAD + 1):
        b = b + kz[k] * v_ref[z + k, :, cols]
    p = p_ref[pz, :, cols]
    if d_ref is None:
        out_ref[to, :, cols] = p / b
    else:
        out_ref[to, :, cols] = p / (b * d_ref[0][d_ref[1], :, cols])
    off = jnp.max(jnp.abs(b - 1.0).reshape(height // ROWS, ROWS, LANES), axis=0)
    dev_ref[...] = jnp.maximum(dev_ref[...], off)


def smear_planes(src, dst, taps, begin, count):
    height = src.shape[1]
    chunk = 2 * ROWS if height % (2 * ROWS) == 0 else ROWS

    def body(z, _):
        for y in range(0, height, chunk):
            dst[z, y : y + chunk, :] = smear_x(src[z, y : y + chunk, :], taps)
        return 0

    lax.fori_loop(begin, begin + count, body, 0)


def inner_kernel(last, *refs):
    if last:
        kernel_ref, p_ref, u_ref, tail_ref, vtop_ref, vbot_ref, d_ref, out_ref, dev_ref, below_ref, above_ref, v = refs
    else:
        kernel_ref, p_ref, u_ref, tail_ref, vtop_ref, vbot_ref, out_ref, unext_ref, dev_ref, below_ref, above_ref, v = refs
        d_ref = None
    planes, height, length = p_ref.shape
    ky = taps_of(kernel_ref, 0)
    kz = taps_of(kernel_ref, 1)
    dev_ref[...] = jnp.zeros_like(dev_ref)
    for z in range(RAD):
        v[z] = vtop_ref[z]
        v[planes - RAD + z] = vbot_ref[z]
    for x in range(0, length, LANES):
        cols = slice(x, x + LANES)

        def smear(z, _, cols=cols):
            column = jnp.concatenate([u_ref[z, :, cols], tail_ref[z, :, cols]], axis=0)
            v[z, :, cols] = smear_y(column, ky, height)
            return 0

        lax.fori_loop(RAD, planes - RAD, smear, 0)

        def body(z, _, cols=cols):
            d_at = None if d_ref is None else (d_ref, z + RAD)
            finish(v, z, cols, kz, p_ref, z + RAD, d_at, out_ref, z + RAD, dev_ref)
            return 0

        lax.fori_loop(0, planes - 2 * RAD, body, 0)
    for z in range(RAD):
        below_ref[z] = v[RAD + z]
        above_ref[z] = v[planes - 2 * RAD + z]
    if not last:
        smear_planes(out_ref, unext_ref, taps_of(kernel_ref, 2), RAD, planes - 2 * RAD)


def edge_kernel(last, *refs):
    kernel_ref, p_ref, zlo_ref, zhi_ref, vtop_ref, vbot_ref, below_ref, above_ref = refs[:8]
    d_ref = None
    if last:
        d_ref, _, whole_ref, dev_ref, v, out_ref, sems = refs[8:]
    else:
        out_ref, unext_ref, dev_ref, v = refs[8:]
    have, height, length = p_ref.shape
    kz = taps_of(kernel_ref, 1)
    dev_ref[...] = jnp.zeros_like(dev_ref)
    copies = []
    for side, parts in enumerate(((zlo_ref, vtop_ref, below_ref), (above_ref, vbot_ref, zhi_ref))):
        p_first = side * (have - RAD)
        first = side * RAD
        d_first = None if d_ref is None else side * (d_ref.shape[0] - RAD)
        for n, part in enumerate(parts):
            for z in range(RAD):
                v[n * RAD + z] = part[z]
        for x in range(0, length, LANES):
            cols = slice(x, x + LANES)

            def body(z, _, cols=cols, p_first=p_first, first=first, d_first=d_first):
                d_at = None if d_ref is None else (d_ref, d_first + z)
                finish(v, z, cols, kz, p_ref, p_first + z, d_at, out_ref, first + z, dev_ref)
                return 0

            lax.fori_loop(0, RAD, body, 0)
        if last:
            copy = pltpu.make_async_copy(
                out_ref.at[pl.ds(first, RAD)], whole_ref.at[pl.ds(d_first, RAD)], sems.at[side]
            )
            copy.start()
            copies.append(copy)
        else:
            smear_planes(out_ref, unext_ref, taps_of(kernel_ref, 2), first, RAD)
    for copy in copies:
        copy.wait()


def from_neighbour(block, axis, step):
    count = lax.axis_size(axis)
    pairs = [(i + step, i) for i in range(count) if 0 <= i + step < count]
    return lax.ppermute(block, axis, pairs)


def max_over(value, axis):
    count = lax.axis_size(axis)
    step = 1
    while step < count:
        value = jnp.maximum(value, lax.ppermute(value, axis, [(i, (i + step) % count) for i in range(count)]))
        step *= 2
    return value


def shards(data_weight, blob_taps):
    kernel = blob_taps / jnp.sum(blob_taps, axis=1, keepdims=True)
    d = jnp.transpose(data_weight, (1, 0, 2))
    planes, height, length = d.shape
    vmem = pl.BlockSpec(memory_space=pltpu.VMEM)
    smem = pl.BlockSpec(memory_space=pltpu.SMEM)
    whole = jax.ShapeDtypeStruct(d.shape, d.dtype)
    rim = jax.ShapeDtypeStruct((RAD, height, length), d.dtype)
    tails = jax.ShapeDtypeStruct((planes, ROWS, length), d.dtype)
    dev_shape = jax.ShapeDtypeStruct((ROWS, LANES), d.dtype)
    params = pltpu.CompilerParams(vmem_limit_bytes=22 * 1024 * 1024)

    anywhere = pl.BlockSpec(memory_space=pl.ANY)
    rims = jax.ShapeDtypeStruct((2 * RAD, height, length), d.dtype)

    def call(body, outs, args, scratch=(), name=None, last_any=False):
        in_specs = [smem] + [vmem] * len(args)
        out_specs = [vmem] * len(outs)
        aliases = {}
        if last_any:
            in_specs[-1] = out_specs[0] = anywhere
            aliases = {len(args): 0}
        return pl.pallas_call(
            body,
            out_shape=outs,
            in_specs=in_specs,
            out_specs=out_specs,
            scratch_shapes=scratch,
            input_output_aliases=aliases,
            compiler_params=params,
            name=name,
        )(kernel, *args)

    (u,) = call(first_kernel, [whole], [d], name="first")
    p = p_rims = d
    u_rims = u
    devs = []
    full_v = [pltpu.VMEM(d.shape, d.dtype)]
    edge_v = [pltpu.VMEM((3 * RAD, height, length), d.dtype)]
    for iteration in range(ITERS):
        last = iteration == ITERS - 1
        if iteration == 0:
            yend, yfirst = u[:, height - RAD :], u[:, :RAD]
        else:
            parts = (u_rims[:RAD], u[RAD : planes - RAD], u_rims[RAD:])
            yend = jnp.concatenate([part[:, height - RAD :] for part in parts], axis=0)
            yfirst = jnp.concatenate([part[:, :RAD] for part in parts], axis=0)
        ylo = from_neighbour(yend, "gy", -1)
        yhi = from_neighbour(yfirst, "gy", 1)
        vtop, vbot, tail = call(rim_kernel, [rim, rim, tails], [u_rims, ylo, yhi], name="rim")
        zlo = from_neighbour(vbot, "gz", -1)
        zhi = from_neighbour(vtop, "gz", 1)
        state = [whole] if last else [whole, whole]
        extra = [d] if last else []
        outs = call(
            functools.partial(inner_kernel, last),
            state + [dev_shape, rim, rim],
            [p, u, tail, vtop, vbot] + extra,
            full_v,
            name="inner",
        )
        fresh, (dev, below, above) = outs[: len(state)], outs[len(state) :]
        args = [p_rims, zlo, zhi, vtop, vbot, below, above]
        if last:
            scratch = edge_v + [pltpu.VMEM(rims.shape, d.dtype), pltpu.SemaphoreType.DMA((2,))]
            weight, edge_dev = call(
                functools.partial(edge_kernel, True), [whole, dev_shape], args + [d, fresh[0]], scratch, "edge", True
            )
        else:
            p, u = fresh
            p_rims, u_rims, edge_dev = call(
                functools.partial(edge_kernel, False), [rims, rims, dev_shape], args, edge_v, "edge"
            )
        devs.append(jnp.maximum(dev, edge_dev))
    local = jnp.max(jnp.stack(devs), axis=(1, 2))
    return jnp.transpose(weight, (1, 0, 2)), max_over(max_over(local, "gz"), "gy")


def solution(mesh):
    return jax.shard_map(
        shards,
        mesh=mesh,
        in_specs=(P("gy", "gz", None), P()),
        out_specs=(P("gy", "gz", None), P()),
        check_vma=False,
    )
```

```python
import functools

import jax
import jax.numpy as jnp
from jax import lax
from jax.experimental import pallas as pl
from jax.experimental.pallas import tpu as pltpu
from jax.sharding import PartitionSpec as P

RAD = 3
ITERS = 3
LANES = 128
ROWS = 8


def smear_cyclic(field, taps, axis):
    length = field.shape[axis]

    def ahead(value, count):
        return pltpu.roll(value, (-count) % length, axis)

    one = ahead(field, 1)
    two = ahead(field, 2)
    low = taps[0] * field + taps[1] * one + taps[2] * two
    mid = taps[3] * field + taps[4] * one + taps[5] * two
    return ahead(low, -RAD) + mid + ahead(taps[6] * field, RAD)


def smear_x(row, taps):
    padded = jnp.concatenate([row, jnp.zeros((row.shape[0], LANES), row.dtype)], axis=1)
    return smear_cyclic(padded, taps, 1)[:, : row.shape[1]]


def smear_x_all(src, dst, taps):
    planes, height, _ = src.shape
    chunk = 2 * ROWS if height % (2 * ROWS) == 0 else ROWS

    def body(z, _):
        for y in range(0, height, chunk):
            dst[z, y : y + chunk, :] = smear_x(src[z, y : y + chunk, :], taps)
        return 0

    lax.fori_loop(0, planes, body, 0)


def first_kernel(kernel_ref, d_ref, u_ref):
    taps = [kernel_ref[2, k] for k in range(2 * RAD + 1)]
    smear_x_all(d_ref, u_ref, taps)


def smear_y(column, taps, height):
    return smear_cyclic(column, taps, 0)[:height]


def taps_of(kernel_ref, row):
    return [kernel_ref[row, k] for k in range(2 * RAD + 1)]


def rim_kernel(raw, kernel_ref, u_ref, ylo_ref, yhi_ref, vtop_ref, vbot_ref, tail_ref):
    planes = tail_ref.shape[0]
    have, height, length = u_ref.shape
    ky = taps_of(kernel_ref, 0)

    def fill(z, _):
        tail_ref[z] = jnp.zeros((ROWS, length), tail_ref.dtype)
        tail_ref[z, 0:RAD, :] = yhi_ref[z]
        tail_ref[z, ROWS - RAD : ROWS, :] = ylo_ref[z]
        if raw:
            tail_ref[z] = smear_x(tail_ref[z], taps_of(kernel_ref, 2))
        return 0

    lax.fori_loop(0, planes, fill, 0)
    for x in range(0, length, LANES):
        cols = slice(x, x + LANES)

        def body(i, _, cols=cols):
            for out, z, t in ((vtop_ref, i, i), (vbot_ref, have - RAD + i, planes - RAD + i)):
                column = jnp.concatenate([u_ref[z, :, cols], tail_ref[t, :, cols]], axis=0)
                out[i, :, cols] = smear_y(column, ky, height)
            return 0

        lax.fori_loop(0, RAD, body, 0)


def finish(v_ref, z, cols, kz, p_ref, pz, d_ref, out_ref, to, dev_ref):
    height = p_ref.shape[1]
    b = kz[0] * v_ref[z, :, cols]
    for k in range(1, 2 * RAD + 1):
        b = b + kz[k] * v_ref[z + k, :, cols]
    p = p_ref[pz, :, cols]
    if d_ref is None:
        out_ref[to, :, cols] = p / b
    else:
        out_ref[to, :, cols] = p / (b * d_ref[0][d_ref[1], :, cols])
    off = jnp.max(jnp.abs(b - 1.0).reshape(height // ROWS, ROWS, LANES), axis=0)
    dev_ref[...] = jnp.maximum(dev_ref[...], off)


def smear_planes(src, dst, taps, begin, count):
    height = src.shape[1]
    chunk = 2 * ROWS if height % (2 * ROWS) == 0 else ROWS

    def body(z, _):
        for y in range(0, height, chunk):
            dst[z, y : y + chunk, :] = smear_x(src[z, y : y + chunk, :], taps)
        return 0

    lax.fori_loop(begin, begin + count, body, 0)


def inner_kernel(last, *refs):
    if last:
        kernel_ref, p_ref, u_ref, tail_ref, vtop_ref, vbot_ref, d_ref, out_ref, dev_ref, below_ref, above_ref, v = refs
    else:
        kernel_ref, p_ref, u_ref, tail_ref, vtop_ref, vbot_ref, out_ref, unext_ref, dev_ref, below_ref, above_ref, v = refs
        d_ref = None
    planes, height, length = p_ref.shape
    ky = taps_of(kernel_ref, 0)
    kz = taps_of(kernel_ref, 1)
    dev_ref[...] = jnp.zeros_like(dev_ref)
    for z in range(RAD):
        v[z] = vtop_ref[z]
        v[planes - RAD + z] = vbot_ref[z]
    for x in range(0, length, LANES):
        cols = slice(x, x + LANES)

        def smear(z, _, cols=cols):
            column = jnp.concatenate([u_ref[z, :, cols], tail_ref[z, :, cols]], axis=0)
            v[z, :, cols] = smear_y(column, ky, height)
            return 0

        lax.fori_loop(RAD, planes - RAD, smear, 0)

        def body(z, _, cols=cols):
            d_at = None if d_ref is None else (d_ref, z + RAD)
            finish(v, z, cols, kz, p_ref, z + RAD, d_at, out_ref, z + RAD, dev_ref)
            return 0

        lax.fori_loop(0, planes - 2 * RAD, body, 0)
    for z in range(RAD):
        below_ref[z] = v[RAD + z]
        above_ref[z] = v[planes - 2 * RAD + z]
    if not last:
        smear_planes(out_ref, unext_ref, taps_of(kernel_ref, 2), RAD, planes - 2 * RAD)


def edge_kernel(last, *refs):
    kernel_ref, p_ref, zlo_ref, zhi_ref, vtop_ref, vbot_ref, below_ref, above_ref = refs[:8]
    d_ref = None
    if last:
        d_ref, _, whole_ref, dev_ref, v, out_ref, sems = refs[8:]
    else:
        out_ref, unext_ref, dev_ref, v = refs[8:]
    have, height, length = p_ref.shape
    kz = taps_of(kernel_ref, 1)
    dev_ref[...] = jnp.zeros_like(dev_ref)
    copies = []
    for side, parts in enumerate(((zlo_ref, vtop_ref, below_ref), (above_ref, vbot_ref, zhi_ref))):
        p_first = side * (have - RAD)
        first = side * RAD
        d_first = None if d_ref is None else side * (d_ref.shape[0] - RAD)
        for n, part in enumerate(parts):
            for z in range(RAD):
                v[n * RAD + z] = part[z]
        for x in range(0, length, LANES):
            cols = slice(x, x + LANES)

            def body(z, _, cols=cols, p_first=p_first, first=first, d_first=d_first):
                d_at = None if d_ref is None else (d_ref, d_first + z)
                finish(v, z, cols, kz, p_ref, p_first + z, d_at, out_ref, first + z, dev_ref)
                return 0

            lax.fori_loop(0, RAD, body, 0)
        if last:
            copy = pltpu.make_async_copy(
                out_ref.at[pl.ds(first, RAD)], whole_ref.at[pl.ds(d_first, RAD)], sems.at[side]
            )
            copy.start()
            copies.append(copy)
        else:
            smear_planes(out_ref, unext_ref, taps_of(kernel_ref, 2), first, RAD)
    for copy in copies:
        copy.wait()


def from_neighbour(block, axis, step):
    count = lax.axis_size(axis)
    pairs = [(i + step, i) for i in range(count) if 0 <= i + step < count]
    return lax.ppermute(block, axis, pairs)


def max_over(value, axis):
    count = lax.axis_size(axis)
    step = 1
    while step < count:
        if count & (count - 1) == 0:
            pairs = [(i, i ^ step) for i in range(count)]
        else:
            pairs = [(i, (i + step) % count) for i in range(count)]
        value = jnp.maximum(value, lax.ppermute(value, axis, pairs))
        step *= 2
    return value


def shards(data_weight, blob_taps):
    kernel = blob_taps / jnp.sum(blob_taps, axis=1, keepdims=True)
    d = jnp.transpose(data_weight, (1, 0, 2))
    planes, height, length = d.shape
    vmem = pl.BlockSpec(memory_space=pltpu.VMEM)
    smem = pl.BlockSpec(memory_space=pltpu.SMEM)
    whole = jax.ShapeDtypeStruct(d.shape, d.dtype)
    rim = jax.ShapeDtypeStruct((RAD, height, length), d.dtype)
    tails = jax.ShapeDtypeStruct((planes, ROWS, length), d.dtype)
    dev_shape = jax.ShapeDtypeStruct((ROWS, LANES), d.dtype)
    params = pltpu.CompilerParams(vmem_limit_bytes=22 * 1024 * 1024)

    anywhere = pl.BlockSpec(memory_space=pl.ANY)
    rims = jax.ShapeDtypeStruct((2 * RAD, height, length), d.dtype)

    def call(body, outs, args, scratch=(), name=None, last_any=False):
        in_specs = [smem] + [vmem] * len(args)
        out_specs = [vmem] * len(outs)
        aliases = {}
        if last_any:
            in_specs[-1] = out_specs[0] = anywhere
            aliases = {len(args): 0}
        return pl.pallas_call(
            body,
            out_shape=outs,
            in_specs=in_specs,
            out_specs=out_specs,
            scratch_shapes=scratch,
            input_output_aliases=aliases,
            compiler_params=params,
            name=name,
        )(kernel, *args)

    (u,) = call(first_kernel, [whole], [d], name="first")
    p = p_rims = d
    u_rims = u
    devs = []
    full_v = [pltpu.VMEM(d.shape, d.dtype)]
    edge_v = [pltpu.VMEM((3 * RAD, height, length), d.dtype)]
    for iteration in range(ITERS):
        last = iteration == ITERS - 1
        if iteration == 0:
            yend, yfirst = d[:, height - RAD :], d[:, :RAD]
        else:
            parts = (u_rims[:RAD], u[RAD : planes - RAD], u_rims[RAD:])
            yend = jnp.concatenate([part[:, height - RAD :] for part in parts], axis=0)
            yfirst = jnp.concatenate([part[:, :RAD] for part in parts], axis=0)
        ylo = from_neighbour(yend, "gy", -1)
        yhi = from_neighbour(yfirst, "gy", 1)
        vtop, vbot, tail = call(functools.partial(rim_kernel, iteration == 0), [rim, rim, tails], [u_rims, ylo, yhi], name="rim")
        zlo = from_neighbour(vbot, "gz", -1)
        zhi = from_neighbour(vtop, "gz", 1)
        state = [whole] if last else [whole, whole]
        extra = [d] if last else []
        outs = call(
            functools.partial(inner_kernel, last),
            state + [dev_shape, rim, rim],
            [p, u, tail, vtop, vbot] + extra,
            full_v,
            name="inner",
        )
        fresh, (dev, below, above) = outs[: len(state)], outs[len(state) :]
        args = [p_rims, zlo, zhi, vtop, vbot, below, above]
        if last:
            scratch = edge_v + [pltpu.VMEM(rims.shape, d.dtype), pltpu.SemaphoreType.DMA((2,))]
            weight, edge_dev = call(
                functools.partial(edge_kernel, True), [whole, dev_shape], args + [d, fresh[0]], scratch, "edge", True
            )
        else:
            p, u = fresh
            p_rims, u_rims, edge_dev = call(
                functools.partial(edge_kernel, False), [rims, rims, dev_shape], args, edge_v, "edge"
            )
        devs.append(jnp.maximum(dev, edge_dev))
    local = jnp.max(jnp.stack(devs), axis=(1, 2))
    return jnp.transpose(weight, (1, 0, 2)), max_over(max_over(local, "gz"), "gy")


def solution(mesh):
    return jax.shard_map(
        shards,
        mesh=mesh,
        in_specs=(P("gy", "gz", None), P()),
        out_specs=(P("gy", "gz", None), P()),
        check_vma=False,
    )
```

```python
import functools

import jax
import jax.numpy as jnp
from jax import lax
from jax.experimental import pallas as pl
from jax.experimental.pallas import tpu as pltpu
from jax.sharding import PartitionSpec as P

RAD = 3
ITERS = 3
LANES = 128
ROWS = 8


def smear_cyclic(field, taps, axis):
    length = field.shape[axis]

    def ahead(value, count):
        return pltpu.roll(value, (-count) % length, axis)

    one = ahead(field, 1)
    two = ahead(field, 2)
    low = taps[0] * field + taps[1] * one + taps[2] * two
    mid = taps[3] * field + taps[4] * one + taps[5] * two
    return ahead(low, -RAD) + mid + ahead(taps[6] * field, RAD)


def band_of(taps, length):
    row = lax.broadcasted_iota(jnp.int32, (length, length), 0)
    col = lax.broadcasted_iota(jnp.int32, (length, length), 1)
    band = jnp.zeros((length, length), taps.dtype)
    for k in range(2 * RAD + 1):
        band = jnp.where(row - col == k - RAD, taps[k], band)
    high = lax.reduce_precision(band, 8, 7)
    return jnp.stack([high.astype(jnp.bfloat16), (band - high).astype(jnp.bfloat16)])


def smear_x(rows, band_ref, store):
    length = rows.shape[1]
    high = rows.astype(jnp.bfloat16)
    low = (rows - high.astype(jnp.float32)).astype(jnp.bfloat16)
    for begin in range(0, length, 2 * LANES):
        end = min(begin + 2 * LANES, length)
        first = max(begin - LANES, 0)
        stop = min(end + LANES, length)

        def product(a, n):
            return jnp.dot(
                a[:, first:stop], band_ref[n, first:stop, begin:end], preferred_element_type=jnp.float32
            )

        store(slice(begin, end), product(high, 0) + product(low, 0) + product(high, 1))


def smear_planes(src, dst, band_ref, begin, count):
    _, height, length = src.shape
    group = max(n for n in range(1, 8) if count % n == 0)

    def body(i, _):
        at = pl.ds(begin + i * group, group)

        def store(cols, value):
            dst[at, :, cols] = value.reshape(group, height, value.shape[1])

        smear_x(src[at].reshape(group * height, length), band_ref, store)
        return 0

    lax.fori_loop(0, count // group, body, 0)


def first_kernel(kernel_ref, d_ref, band_ref, u_ref):
    smear_planes(d_ref, u_ref, band_ref, 0, d_ref.shape[0])


def smear_y(column, taps, height):
    return smear_cyclic(column, taps, 0)[:height]


def taps_of(kernel_ref, row):
    return [kernel_ref[row, k] for k in range(2 * RAD + 1)]


def rim_kernel(raw, kernel_ref, u_ref, ylo_ref, yhi_ref, *refs):
    vtop_ref, vbot_ref, tail_ref = refs[-3:]
    planes = tail_ref.shape[0]
    have, height, length = u_ref.shape
    ky = taps_of(kernel_ref, 0)

    def fill(z, _):
        tail_ref[z] = jnp.zeros((ROWS, length), tail_ref.dtype)
        tail_ref[z, 0:RAD, :] = yhi_ref[z]
        tail_ref[z, ROWS - RAD : ROWS, :] = ylo_ref[z]
        return 0

    lax.fori_loop(0, planes, fill, 0)
    if raw:
        smear_planes(tail_ref, tail_ref, refs[0], 0, planes)
    for x in range(0, length, LANES):
        cols = slice(x, x + LANES)

        def body(i, _, cols=cols):
            for out, z, t in ((vtop_ref, i, i), (vbot_ref, have - RAD + i, planes - RAD + i)):
                column = jnp.concatenate([u_ref[z, :, cols], tail_ref[t, :, cols]], axis=0)
                out[i, :, cols] = smear_y(column, ky, height)
            return 0

        lax.fori_loop(0, RAD, body, 0)


def finish(v_ref, z, cols, kz, p_ref, pz, d_ref, out_ref, to, dev_ref):
    height = p_ref.shape[1]
    b = kz[0] * v_ref[z, :, cols]
    for k in range(1, 2 * RAD + 1):
        b = b + kz[k] * v_ref[z + k, :, cols]
    p = p_ref[pz, :, cols]
    if d_ref is None:
        out_ref[to, :, cols] = p / b
    else:
        out_ref[to, :, cols] = p / (b * d_ref[0][d_ref[1], :, cols])
    off = jnp.max(jnp.abs(b - 1.0).reshape(height // ROWS, ROWS, LANES), axis=0)
    dev_ref[...] = jnp.maximum(dev_ref[...], off)


def inner_kernel(last, *refs):
    if last:
        kernel_ref, p_ref, u_ref, tail_ref, vtop_ref, vbot_ref, d_ref, out_ref, dev_ref, below_ref, above_ref, v = refs
    else:
        kernel_ref, p_ref, u_ref, tail_ref, vtop_ref, vbot_ref, band_ref, out_ref, unext_ref, dev_ref, below_ref, above_ref, v = refs
        d_ref = None
    planes, height, length = p_ref.shape
    ky = taps_of(kernel_ref, 0)
    kz = taps_of(kernel_ref, 1)
    dev_ref[...] = jnp.zeros_like(dev_ref)
    for z in range(RAD):
        v[z] = vtop_ref[z]
        v[planes - RAD + z] = vbot_ref[z]
    for x in range(0, length, LANES):
        cols = slice(x, x + LANES)

        def smear(z, _, cols=cols):
            column = jnp.concatenate([u_ref[z, :, cols], tail_ref[z, :, cols]], axis=0)
            v[z, :, cols] = smear_y(column, ky, height)
            return 0

        lax.fori_loop(RAD, planes - RAD, smear, 0)

        def body(z, _, cols=cols):
            d_at = None if d_ref is None else (d_ref, z + RAD)
            finish(v, z, cols, kz, p_ref, z + RAD, d_at, out_ref, z + RAD, dev_ref)
            return 0

        lax.fori_loop(0, planes - 2 * RAD, body, 0)
    for z in range(RAD):
        below_ref[z] = v[RAD + z]
        above_ref[z] = v[planes - 2 * RAD + z]
    if not last:
        smear_planes(out_ref, unext_ref, band_ref, RAD, planes - 2 * RAD)


def edge_kernel(last, *refs):
    kernel_ref, p_ref, zlo_ref, zhi_ref, vtop_ref, vbot_ref, below_ref, above_ref = refs[:8]
    d_ref = None
    if last:
        d_ref, _, whole_ref, dev_ref, v, out_ref, sems = refs[8:]
    else:
        band_ref, out_ref, unext_ref, dev_ref, v = refs[8:]
    have, height, length = p_ref.shape
    kz = taps_of(kernel_ref, 1)
    dev_ref[...] = jnp.zeros_like(dev_ref)
    copies = []
    for side, parts in enumerate(((zlo_ref, vtop_ref, below_ref), (above_ref, vbot_ref, zhi_ref))):
        p_first = side * (have - RAD)
        first = side * RAD
        d_first = None if d_ref is None else side * (d_ref.shape[0] - RAD)
        for n, part in enumerate(parts):
            for z in range(RAD):
                v[n * RAD + z] = part[z]
        for x in range(0, length, LANES):
            cols = slice(x, x + LANES)

            def body(z, _, cols=cols, p_first=p_first, first=first, d_first=d_first):
                d_at = None if d_ref is None else (d_ref, d_first + z)
                finish(v, z, cols, kz, p_ref, p_first + z, d_at, out_ref, first + z, dev_ref)
                return 0

            lax.fori_loop(0, RAD, body, 0)
        if last:
            copy = pltpu.make_async_copy(
                out_ref.at[pl.ds(first, RAD)], whole_ref.at[pl.ds(d_first, RAD)], sems.at[side]
            )
            copy.start()
            copies.append(copy)
        else:
            smear_planes(out_ref, unext_ref, band_ref, first, RAD)
    for copy in copies:
        copy.wait()


def from_neighbour(block, axis, step):
    count = lax.axis_size(axis)
    pairs = [(i + step, i) for i in range(count) if 0 <= i + step < count]
    return lax.ppermute(block, axis, pairs)


def max_over(value, axis):
    count = lax.axis_size(axis)
    step = 1
    while step < count:
        if count & (count - 1) == 0:
            pairs = [(i, i ^ step) for i in range(count)]
        else:
            pairs = [(i, (i + step) % count) for i in range(count)]
        value = jnp.maximum(value, lax.ppermute(value, axis, pairs))
        step *= 2
    return value


def shards(data_weight, blob_taps):
    kernel = blob_taps / jnp.sum(blob_taps, axis=1, keepdims=True)
    d = jnp.transpose(data_weight, (1, 0, 2))
    planes, height, length = d.shape
    vmem = pl.BlockSpec(memory_space=pltpu.VMEM)
    smem = pl.BlockSpec(memory_space=pltpu.SMEM)
    whole = jax.ShapeDtypeStruct(d.shape, d.dtype)
    rim = jax.ShapeDtypeStruct((RAD, height, length), d.dtype)
    tails = jax.ShapeDtypeStruct((planes, ROWS, length), d.dtype)
    dev_shape = jax.ShapeDtypeStruct((ROWS, LANES), d.dtype)
    params = pltpu.CompilerParams(vmem_limit_bytes=22 * 1024 * 1024)

    anywhere = pl.BlockSpec(memory_space=pl.ANY)
    rims = jax.ShapeDtypeStruct((2 * RAD, height, length), d.dtype)

    def call(body, outs, args, scratch=(), name=None, last_any=False):
        in_specs = [smem] + [vmem] * len(args)
        out_specs = [vmem] * len(outs)
        aliases = {}
        if last_any:
            in_specs[-1] = out_specs[0] = anywhere
            aliases = {len(args): 0}
        return pl.pallas_call(
            body,
            out_shape=outs,
            in_specs=in_specs,
            out_specs=out_specs,
            scratch_shapes=scratch,
            input_output_aliases=aliases,
            compiler_params=params,
            name=name,
        )(kernel, *args)

    band = band_of(kernel[2], length)
    (u,) = call(first_kernel, [whole], [d, band], name="first")
    p = p_rims = d
    u_rims = u
    devs = []
    full_v = [pltpu.VMEM(d.shape, d.dtype)]
    edge_v = [pltpu.VMEM((3 * RAD, height, length), d.dtype)]
    for iteration in range(ITERS):
        last = iteration == ITERS - 1
        if iteration == 0:
            yend, yfirst = d[:, height - RAD :], d[:, :RAD]
        else:
            parts = (u_rims[:RAD], u[RAD : planes - RAD], u_rims[RAD:])
            yend = jnp.concatenate([part[:, height - RAD :] for part in parts], axis=0)
            yfirst = jnp.concatenate([part[:, :RAD] for part in parts], axis=0)
        ylo = from_neighbour(yend, "gy", -1)
        yhi = from_neighbour(yfirst, "gy", 1)
        vtop, vbot, tail = call(functools.partial(rim_kernel, iteration == 0), [rim, rim, tails], [u_rims, ylo, yhi] + ([band] if iteration == 0 else []), name="rim")
        zlo = from_neighbour(vbot, "gz", -1)
        zhi = from_neighbour(vtop, "gz", 1)
        state = [whole] if last else [whole, whole]
        extra = [d] if last else [band]
        outs = call(
            functools.partial(inner_kernel, last),
            state + [dev_shape, rim, rim],
            [p, u, tail, vtop, vbot] + extra,
            full_v,
            name="inner",
        )
        fresh, (dev, below, above) = outs[: len(state)], outs[len(state) :]
        args = [p_rims, zlo, zhi, vtop, vbot, below, above]
        if last:
            scratch = edge_v + [pltpu.VMEM(rims.shape, d.dtype), pltpu.SemaphoreType.DMA((2,))]
            weight, edge_dev = call(
                functools.partial(edge_kernel, True), [whole, dev_shape], args + [d, fresh[0]], scratch, "edge", True
            )
        else:
            p, u = fresh
            p_rims, u_rims, edge_dev = call(
                functools.partial(edge_kernel, False), [rims, rims, dev_shape], args + [band], edge_v, "edge"
            )
        devs.append(jnp.maximum(dev, edge_dev))
    local = jnp.max(jnp.stack(devs), axis=(1, 2))
    return jnp.transpose(weight, (1, 0, 2)), max_over(max_over(local, "gz"), "gy")


def solution(mesh):
    return jax.shard_map(
        shards,
        mesh=mesh,
        in_specs=(P("gy", "gz", None), P()),
        out_specs=(P("gy", "gz", None), P()),
        check_vma=False,
    )
```
